32 devices in a mesh: mesh: 16 (over z, y, core), mem: 2 (over x).
Axes of the slice: x: 2, y: 2, z: 4, core: 2. Of those that a mesh axis runs over, the one named last changes fastest.
Arguments:
- ensemble: bfloat16 [40, 240, 6144], P('mem', None, 'mesh'), may hold values from -6 to 6
- ovl_owner: int32 [384, 2], P('mesh'), may hold values from 0 to 15, all different within a row; in each aligned block of 24 rows (0 to 23, 24 to 47, ...) at most 5 rows name the same one
- ovl_patch: int32 [384, 2], P('mesh'), may hold values from 0 to 7
- ovl_weight: bfloat16 [384, 2, 16, 8], P('mesh'), may hold values from 0.0099487305 to 0.19921875
- letkf_weight: float32 [16, 40, 40], P('mesh'), may hold values from -1 to 1
Outputs:
- analysis: bfloat16 [40, 240, 6144], P('mem', None, 'mesh')
The draws below stay inside these ranges and needn't reach their ends.
Inputs may be any that keep to these rules, and one draw needn't show every extreme that they name: `ovl_owner`: within the 24 rows of one mesh index, the two entries of a row differ, and each owner is named at most 5 times; some owner exactly 5 times.
All inputs are finite; a program needn't handle non-finite values.
Results may differ from the reference program's by a relative error of at most 0.0015.
Values may be sent and summed in bfloat16 or wider, within the bound.
A program may use at most 128 MiB of HBM per device.

```python
import math
import jax
import jax.numpy as jnp
import numpy as np
from jax import lax

M = 40
C = 240
BE = 16
PG = 8
PATCH_TILE = 8
NBLK = 24
NPATCH_DEV = 8
CAP = 5
ELEMS = 6144
BLOCKS = 384
TILES = 16
N_MESH = 16


def touch_ends(entries, stream_key, low, top_value):
    dims = entries.shape
    place = [jax.random.randint(jax.random.fold_in(stream_key, axis), (), 0, dims[axis]) for axis in range(len(dims))]
    entries = entries.at[tuple(place)].set(low)
    longest = dims.index(max(dims))
    place[longest] = (place[longest] + 1) % dims[longest]
    return entries.at[tuple(place)].set(top_value)


def levels(own_key, dims, cuts, least, top_value):
    level = 1.0
    for position, shards_of in cuts:
        draws = jax.random.uniform(jax.random.fold_in(jax.random.fold_in(own_key, 6), position), (shards_of,), jnp.float32, least / len(cuts), top_value / len(cuts))
        level = level * jnp.repeat(jnp.exp(draws), dims[position] // shards_of).reshape((-1,) + (1,) * (len(dims) - 1 - position))
    return level


def routed_block(stream_key, own, number, rows, number_of, top, most, lean):
    ranking = jax.random.permutation(stream_key, number_of)
    heavy_load, usual = load_shares(number_of, rows * top, most, lean, True), load_shares(number_of, rows * top, most, lean, False)
    places = jnp.arange(number_of)

    def named(sizes, rotation):
        used = int((sizes > 0).sum())
        fixed = max(1, used // 4)
        passed = fixed + (places - fixed + rotation * (used - fixed)) % max(1, number_of - fixed)
        return jnp.zeros((number_of,), jnp.int32).at[ranking[jnp.where(places < fixed, places, passed)]].set(jnp.asarray(sizes, jnp.int32))

    sizes = jnp.where(number % 4 == 0, named(heavy_load, number // 4), named(usual, number - number // 4 - 1))
    mixed = jax.random.permutation(jax.random.fold_in(own, 3), number_of)
    source_of, sink = mixed[0:number_of // 2 * 2:2], mixed[1:number_of // 2 * 2:2]
    room = jnp.minimum(sizes[source_of] - 1, most - sizes[sink]) // 2
    room = jnp.where((source_of == ranking[0]) | (sink == ranking[0]) | (sizes[sink] == 0), 0, jnp.maximum(room, 0))
    passed = jax.random.randint(jax.random.fold_in(own, 4), (number_of // 2,), 0, 1 << 20) % (room + 1)
    sizes = sizes.at[source_of].add(-passed).at[sink].add(passed)
    items = jnp.searchsorted(jnp.cumsum(sizes), jnp.arange(rows * top), side="right").astype(jnp.int32)
    grid = items.reshape(top, rows).T
    grid = grid[jax.random.permutation(jax.random.fold_in(own, 1), rows)]
    rotation = jax.random.randint(jax.random.fold_in(own, 2), (rows, 1), 0, top)
    return jnp.take_along_axis(grid, (jnp.arange(top)[None, :] + rotation) % top, axis=1)


def load_shares(amount, total, limit, slope, full):
    loads = [(1 << 20) // math.isqrt(rank ** slope) + 1 for rank in range(1, amount + 1)]
    largest = limit if full else min(limit, max(-(-total // amount), total * loads[0] // sum(loads)))
    least = 1 if total - largest >= amount - 1 else 0
    given, rest = [largest] + [least] * (amount - 1), total - largest - least * (amount - 1)
    while rest > 0:
        free = [i for i in range(1, amount) if given[i] < largest] or [i for i in range(1, amount) if given[i] < limit]
        pool, remaining = sum([loads[i] for i in free]), rest
        for i in free:
            addition = min(limit - given[i], max(1, remaining * loads[i] // pool), rest)
            given[i] = given[i] + addition
            rest = rest - addition
    return np.array(given)


def scatter_about(own_key, dims, scale, limit, split=(), held_as=jnp.bfloat16):
    loudness = levels(own_key, dims, split, -0.22, 0.18) if split else 1.0
    entries = jax.random.normal(own_key, dims, jnp.float32) * scale * loudness
    return jnp.minimum(jnp.maximum(entries, -limit), limit).astype(held_as)


def setup_inputs(seed: int = 0) -> dict:
    streams_of = jax.random.split(jax.random.key(seed), 6)
    ensemble = scatter_about(streams_of[0], (M, C, ELEMS), 1.0, 6.0, ((0, 2), (2, 16)))
    ovl_owner_keys = jax.random.split(jax.random.fold_in(streams_of[1], 1), BLOCKS // NBLK)
    ovl_owner_turns = jax.random.permutation(jax.random.fold_in(streams_of[1], 3), BLOCKS // NBLK)
    ovl_owner = jax.vmap(lambda own, number: routed_block(jax.random.fold_in(streams_of[1], 2), own, number, NBLK, N_MESH, 2, CAP, 2))(ovl_owner_keys, ovl_owner_turns).reshape((BLOCKS, 2))
    ovl_patch = touch_ends(jax.random.randint(streams_of[2], (BLOCKS, 2), 0, NPATCH_DEV), jax.random.fold_in(streams_of[2], 1), 0, NPATCH_DEV - 1).astype(jnp.int32)
    ovl_weight = jnp.clip(jnp.exp(math.log(0.19921875) - 2.9969585 * jax.random.uniform(streams_of[3], (BLOCKS, 2, BE, PG), jnp.float32) ** levels(streams_of[3], (BLOCKS, 2, BE, PG), ((0, 16),), -0.2, 0.2)), 0.0099487305, 0.19921875).astype(jnp.bfloat16)
    letkf_weight = scatter_about(streams_of[4], (TILES, M, M), M ** -0.5, 1.0, ((0, 16),), jnp.float32)
    return {"ensemble": ensemble, "ovl_owner": ovl_owner, "ovl_patch": ovl_patch, "ovl_weight": ovl_weight, "letkf_weight": letkf_weight}


def reference(ensemble, ovl_owner, ovl_patch, ovl_weight, letkf_weight):
    patch_total = N_MESH * NPATCH_DEV
    destination = (ovl_owner * NPATCH_DEV + ovl_patch).astype(jnp.int32)
    blocks_x = ensemble.reshape(M, C, N_MESH, NBLK, BE)

    def forward(carry, device):
        patch_sums, coverage = carry
        device_blocks = lax.dynamic_index_in_dim(blocks_x, device, 2, keepdims=False)
        device_margin = lax.dynamic_slice_in_dim(ovl_weight, device * NBLK, NBLK, 0)
        device_dest = lax.dynamic_slice_in_dim(destination, device * NBLK, NBLK, 0).reshape(-1)
        pieces = jnp.einsum('mcbe,bkeg->bkmcg', device_blocks.astype(jnp.float32), device_margin.astype(jnp.float32)).astype(jnp.bfloat16)
        patch_sums = patch_sums.at[device_dest].add(pieces.reshape(-1, M, C, PG).astype(jnp.float32))
        column_sums = jnp.sum(device_margin.astype(jnp.float32), axis=2).reshape(-1, PG)
        coverage = coverage.at[device_dest].add(column_sums)
        return (patch_sums, coverage), None

    start_sums = jnp.zeros((patch_total, M, C, PG), jnp.float32)
    start_cover = jnp.zeros((patch_total, PG), jnp.float32)
    devices = jnp.arange(N_MESH, dtype=jnp.int32)
    (patch_sums, coverage), _ = lax.scan(forward, (start_sums, start_cover), devices)
    grid_field = (patch_sums / jnp.maximum(coverage, 1.0)[:, None, None, :]).astype(jnp.bfloat16)
    tile_view = grid_field.reshape(TILES, PATCH_TILE, M, C, PG).astype(jnp.float32)
    mixed = jnp.einsum('tjmcg,tmn->tjncg', tile_view, letkf_weight, precision=lax.Precision.HIGHEST)
    increment = (mixed - tile_view).astype(jnp.bfloat16).reshape(patch_total, M, C, PG)

    def backward(carry, device):
        device_blocks = lax.dynamic_index_in_dim(blocks_x, device, 2, keepdims=False)
        device_margin = lax.dynamic_slice_in_dim(ovl_weight, device * NBLK, NBLK, 0).astype(jnp.float32)
        device_dest = lax.dynamic_slice_in_dim(destination, device * NBLK, NBLK, 0).reshape(-1)
        gathered = jnp.take(increment, device_dest, axis=0).reshape(NBLK, 2, M, C, PG)
        element_area = jnp.sum(device_margin, axis=(1, 3))
        correction = jnp.einsum('bkmcg,bkeg->mcbe', gathered.astype(jnp.float32), device_margin) / element_area[None, None]
        updated = (device_blocks.astype(jnp.float32) + correction).astype(jnp.bfloat16)
        return carry, updated

    _, stacked = lax.scan(backward, jnp.zeros((), jnp.float32), devices)
    return jnp.transpose(stacked, (1, 2, 0, 3, 4)).reshape(M, C, N_MESH * NBLK * BE)
```

```python
import jax
import jax.numpy as jnp
from jax import lax
from jax.sharding import PartitionSpec as P

PATCH_TILE = 8


def shards(ensemble, ovl_owner, ovl_patch, ovl_weight, letkf_weight):
    members, channels, element_count = ensemble.shape
    block_count = ovl_owner.shape[0]
    block_size = ovl_weight.shape[2]
    cell_count = ovl_weight.shape[3]
    tile_count = letkf_weight.shape[0]
    own_patches = tile_count * PATCH_TILE
    peer_count = lax.axis_size("mesh")
    patch_total = own_patches * peer_count
    width = members * channels
    flat = ensemble.reshape(width, element_count)

    dest = ovl_owner * own_patches + ovl_patch
    dest_elems = jnp.repeat(dest.T, block_size, axis=1)
    weight = ovl_weight.transpose(1, 3, 0, 2).reshape(2, cell_count, element_count)
    hits = jnp.arange(patch_total, dtype=jnp.int32)[None, :, None] == dest_elems[:, None, :]
    area = jnp.where(hits[0][:, None, :], weight[0][None], 0) + jnp.where(
        hits[1][:, None, :], weight[1][None], 0
    )
    area = area.reshape(patch_total * cell_count, element_count)

    cover_part = jnp.sum(area.astype(jnp.float32), axis=1)
    coverage = lax.psum_scatter(cover_part, "mesh", scatter_dimension=0, tiled=True)

    sums_part = lax.dot_general(
        area, flat, (((1,), (1,)), ((), ())), preferred_element_type=jnp.float32
    ).astype(jnp.bfloat16)
    patch_sums = lax.psum_scatter(sums_part, "mesh", scatter_dimension=0, tiled=True)
    grid_field = (patch_sums.astype(jnp.float32) / jnp.maximum(coverage, 1.0)[:, None]).astype(
        jnp.bfloat16
    )
    tile_view = grid_field.reshape(tile_count, PATCH_TILE * cell_count, members, channels)
    own_start = lax.axis_index("mem") * members
    own_cols = lax.dynamic_slice_in_dim(letkf_weight, own_start, members, 2)
    mixed = jnp.einsum(
        "trmc,tmn->trnc",
        lax.all_gather(tile_view, "mem", axis=2, tiled=True).astype(jnp.float32),
        own_cols,
        precision=lax.Precision.HIGHEST,
    )
    increment = (mixed - tile_view.astype(jnp.float32)).astype(jnp.bfloat16)
    everywhere = lax.all_gather(
        increment.reshape(own_patches * cell_count, width), "mesh", axis=0, tiled=True
    )
    element_area = jnp.sum(weight.astype(jnp.float32), axis=(0, 1))
    correction = lax.dot_general(
        everywhere, area, (((0,), (0,)), ((), ())), preferred_element_type=jnp.float32
    )
    updated = (flat.astype(jnp.float32) + correction / element_area[None]).astype(jnp.bfloat16)
    return updated.reshape(members, channels, element_count)


def solution(mesh):
    in_specs = (
        P("mem", None, "mesh"),
        P("mesh", None),
        P("mesh", None),
        P("mesh", None, None, None),
        P("mesh", None, None),
    )
    out_specs = P("mem", None, "mesh")
    return jax.shard_map(shards, mesh=mesh, in_specs=in_specs, out_specs=out_specs, check_vma=False)
```
